256 devices in a mesh: req: 64 (over y, z, core), rep: 4 (over x).
Axes of the slice: x: 4, y: 4, z: 8, core: 2. Of those that a mesh axis runs over, the one named last changes fastest.
Arguments:
- stream: bfloat16 [32768, 2048], P(('rep', 'req')), parts along dimension 0, may hold values from -6 to 6
- gain: bfloat16 [2048], replicated, may hold values from 0.25 to 1.75
- routes: int32 [32768, 6], P(('rep', 'req')), parts along dimension 0, may hold values from 0 to 63, all different within a row; in each aligned block of 128 rows (0 to 127, 128 to 255, ...) at most 16 rows name the same one
- route_weights: float32 [32768, 6], P(('rep', 'req')), parts along dimension 0, may hold values from 0.05 to 0.45
- placement: int32 [64], replicated, may hold values from 0 to 63, each once
- request_lengths: int32 [2048], P(('rep', 'req')), parts along dimension 0, may hold values from 1 to 121, as said below
- slot_w_in: bfloat16 [64, 2048, 1536], P('req'), may hold values from -0.125 to 0.125
- slot_w_out: bfloat16 [64, 768, 2048], P('req'), may hold values from -0.21875 to 0.21875
Outputs:
- output: bfloat16 [32768, 2048], P(('rep', 'req')), parts along dimension 0
The draws below stay inside these ranges and needn't reach their ends.
There are 4 independent parts, one for each index of `rep`. The reference program is written for one: setup_inputs(seed, part) draws one part's arguments, and reference() takes and returns one part's arrays. A program takes and returns all parts, laid end to end along the dimension named above; an argument that names none is the same for every part. Nothing has to cross between parts.
Inputs may be any that keep to these rules, and one draw needn't show every extreme that they name: `routes`: within the rows of one device (aligned blocks of 128 rows) no expert is named by more than 16 rows, a bound that some block reaches. `placement`: every slot holds exactly one expert. `request_lengths`: each device has 8 requests; the first 7 are single-row decodes; a device's lengths sum to between 64 and 128, and to exactly 128 on some device.
All inputs are finite; a program needn't handle non-finite values.
Results may differ from the reference program's by a relative error of at most 0.005.
Values may be sent and summed in bfloat16 or wider, within the bound.
No kernel may reach another device: no remote copies, remote signals or barrier semaphores. Data moves between devices by JAX's collectives and lax.ppermute only.
A program may use at most 64 MiB of HBM per device.

```python
import math
import jax
import jax.numpy as jnp
import numpy as np
from jax import lax

D = 2048
FF = 768
TOP = 6
ROWS_DEV = 128
REQS_DEV = 8
EXPERTS = 64
CAP = 16
TOKENS = 8192
REQS = 512
N_REQ = 64


def draw_request_lengths(key, part):
    devices = REQS // REQS_DEV
    base_key, pick_key = jax.random.split(jax.random.fold_in(key, 11))
    totals = jax.random.randint(base_key, (devices,), ROWS_DEV // 2, ROWS_DEV + 1)
    fullest = jax.random.randint(pick_key, (), 0, devices)
    totals = jnp.where(jnp.arange(devices) == fullest, ROWS_DEV, totals).astype(jnp.int32)
    decodes = jnp.ones((devices, REQS_DEV - 1), jnp.int32)
    prompts = (totals - (REQS_DEV - 1))[:, None].astype(jnp.int32)
    return jnp.concatenate([decodes, prompts], axis=1).reshape(-1).astype(jnp.int32)


def steps_of(stream_key, extent, cuts, least, top_value):
    loudness, own = 1.0, jax.random.fold_in(stream_key, 6)
    for dim, blocks in cuts:
        heights = jnp.exp(jax.random.uniform(jax.random.fold_in(own, dim), (blocks,), jnp.float32, least / len(cuts), top_value / len(cuts)))
        loudness = loudness * jnp.repeat(heights, extent[dim] // blocks).reshape([-1 if axis == dim else 1 for axis in range(len(extent))])
    return loudness


def routed_block(own_key, own, number, rows, count, top, most, skew):
    order = jax.random.permutation(own_key, count)
    heavy_load, usual = load_shares(count, rows * top, most, skew, True), load_shares(count, rows * top, most, skew, False)
    places = jnp.arange(count)

    def named(tallies, turn):
        used = int((tallies > 0).sum())
        fixed = max(1, used // 4)
        passed = fixed + (places - fixed + turn * (used - fixed)) % max(1, count - fixed)
        return jnp.zeros((count,), jnp.int32).at[order[jnp.where(places < fixed, places, passed)]].set(jnp.asarray(tallies, jnp.int32))

    tallies = jnp.where(number % 4 == 0, named(heavy_load, number // 4), named(usual, number - number // 4 - 1))
    mixed = jax.random.permutation(jax.random.fold_in(own, 3), count)
    giver, receiver = mixed[0:count // 2 * 2:2], mixed[1:count // 2 * 2:2]
    slack = jnp.minimum(tallies[giver] - 1, most - tallies[receiver]) // 2
    slack = jnp.where((giver == order[0]) | (receiver == order[0]) | (tallies[receiver] == 0), 0, jnp.maximum(slack, 0))
    passed = jax.random.randint(jax.random.fold_in(own, 4), (count // 2,), 0, 1 << 20) % (slack + 1)
    tallies = tallies.at[giver].add(-passed).at[receiver].add(passed)
    members = jnp.searchsorted(jnp.cumsum(tallies), jnp.arange(rows * top), side="right").astype(jnp.int32)
    table = members.reshape(top, rows).T
    table = table[jax.random.permutation(jax.random.fold_in(own, 1), rows)]
    turn = jax.random.randint(jax.random.fold_in(own, 2), (rows, 1), 0, top)
    return jnp.take_along_axis(table, (jnp.arange(top)[None, :] + turn) % top, axis=1)


def load_shares(number_of, total, limit, slope, full):
    loads = [(1 << 20) // math.isqrt(grade ** slope) + 1 for grade in range(1, number_of + 1)]
    largest = limit if full else min(limit, max(-(-total // number_of), total * loads[0] // sum(loads)))
    least = 1 if total - largest >= number_of - 1 else 0
    holding, rest = [largest] + [least] * (number_of - 1), total - largest - least * (number_of - 1)
    while rest > 0:
        movable = [i for i in range(1, number_of) if holding[i] < largest] or [i for i in range(1, number_of) if holding[i] < limit]
        pool, left = sum([loads[i] for i in movable]), rest
        for i in movable:
            more = min(limit - holding[i], max(1, left * loads[i] // pool), rest)
            holding[i] = holding[i] + more
            rest = rest - more
    return np.array(holding)


def bell_draw(rng, extent, spread, limit, cuts=(), kind=jnp.bfloat16):
    values = jax.random.normal(rng, extent, jnp.float32) * spread
    if len(cuts) > 0:
        values = steps_of(rng, extent, cuts, -0.22, 0.18) * values
    return jnp.clip(values, min=-limit, max=limit).astype(kind)


def setup_inputs(seed: int = 0, part: int = 0) -> dict:
    key_list = jax.random.split(jax.random.key(seed), 9)
    own_keys = jax.random.split(jax.random.fold_in(key_list[8], part), 9)
    stream = bell_draw(own_keys[0], (TOKENS, D), 1.0, 6.0, ((0, 64),))
    gain = jnp.clip(1.0 + 0.15 * jax.random.normal(key_list[1], (D,), jnp.float32), 0.25, 1.75).astype(jnp.bfloat16)
    routes_keys = jax.random.split(jax.random.fold_in(own_keys[2], 1), TOKENS // ROWS_DEV)
    routes_turns = jax.random.permutation(jax.random.fold_in(own_keys[2], 3), TOKENS // ROWS_DEV)
    routes = jax.vmap(lambda own, number: routed_block(jax.random.fold_in(own_keys[2], 2), own, number, ROWS_DEV, EXPERTS, TOP, CAP, 2))(routes_keys, routes_turns).reshape((TOKENS, TOP))
    route_weights = jnp.clip(0.05 + 0.39999999 * jax.random.uniform(own_keys[3], (TOKENS, TOP), jnp.float32) ** steps_of(own_keys[3], (TOKENS, TOP), ((0, 64),), -0.2, 0.2), 0.05, 0.45)
    placement = jax.random.permutation(key_list[4], EXPERTS).astype(jnp.int32)
    request_lengths = draw_request_lengths(jax.random.fold_in(jax.random.fold_in(key_list[8], part), 71), part)
    slot_w_in = bell_draw(key_list[6], (EXPERTS, D, 2 * FF), D ** -0.5, 0.125, ((0, 64),))
    slot_w_out = bell_draw(key_list[7], (EXPERTS, FF, D), FF ** -0.5, 0.21875, ((0, 64),))
    return {"stream": stream, "gain": gain, "routes": routes, "route_weights": route_weights, "placement": placement, "request_lengths": request_lengths, "slot_w_in": slot_w_in, "slot_w_out": slot_w_out}


EPS = 1e-06

def reference(stream, gain, routes, route_weights, placement, request_lengths, slot_w_in, slot_w_out):
    tokens_all, features = stream.shape
    routed = routes.shape[1]
    slot_count = slot_w_in.shape[0]
    hidden_units = slot_w_out.shape[1]
    stream_wide = stream.astype(jnp.float32)
    inverse = lax.rsqrt(lax.optimization_barrier(jnp.mean(stream_wide * stream_wide, axis=-1, keepdims=True)) + EPS)
    normed = (stream_wide * inverse * gain.astype(jnp.float32)).astype(jnp.bfloat16)
    totals = lax.optimization_barrier(jnp.sum(request_lengths.reshape(N_REQ, REQS_DEV), axis=1)).astype(jnp.int32)
    row_index = jnp.arange(tokens_all, dtype=jnp.int32)
    live_rows = row_index % ROWS_DEV < totals[row_index // ROWS_DEV]
    target = placement[routes].reshape(-1)
    taken_rows = jnp.repeat(live_rows, routed)
    weights_flat = route_weights.reshape(-1)
    slot_limit = N_REQ * CAP

    def one_slot(mixture, inputs):
        slot_id, w_in, w_out = inputs
        chosen_mask = (target == slot_id) & taken_rows
        chosen = jnp.nonzero(chosen_mask, size=slot_limit, fill_value=0)[0].astype(jnp.int32)
        filled = jnp.arange(slot_limit, dtype=jnp.int32) < jnp.sum(chosen_mask.astype(jnp.int32))
        picked = normed[chosen // routed]
        hidden = jnp.dot(picked, w_in, preferred_element_type=jnp.float32)
        activated = (jax.nn.silu(hidden[:, :hidden_units]) * hidden[:, hidden_units:]).astype(jnp.bfloat16)
        result = jnp.dot(activated, w_out, preferred_element_type=jnp.float32).astype(jnp.bfloat16)
        weight = weights_flat[chosen] * filled.astype(jnp.float32)
        mixture = mixture.at[chosen // routed].add(result.astype(jnp.float32) * weight[:, None])
        return (mixture, None)
    mixture, _ = lax.scan(one_slot, jnp.zeros((tokens_all, features), jnp.float32), (jnp.arange(slot_count, dtype=jnp.int32), slot_w_in, slot_w_out))
    return jnp.where(live_rows[:, None], stream_wide + mixture, 0.0).astype(jnp.bfloat16)
```

```python
import jax
import jax.numpy as jnp
from jax import lax
from jax.sharding import PartitionSpec as P

EPS = 1e-06
NY, NZ, NC = 4, 8, 2
CAP = 16
BF = jnp.bfloat16
F32 = jnp.float32


def _index(y, z, c):
    return ((y % NY) * NZ + z % NZ) * NC + c % NC


def _shift(dy=0, dz=0, dc=0):
    return [
        (_index(y, z, c), _index(y + dy, z + dz, c + dc))
        for y in range(NY)
        for z in range(NZ)
        for c in range(NC)
    ]


def _send(x, **by):
    return lax.ppermute(x, "req", _shift(**by))


def expert_block(rows, w_in, w_out):
    hidden = jnp.dot(rows, w_in, preferred_element_type=F32)
    units = w_out.shape[0]
    activated = (jax.nn.silu(hidden[:, :units]) * hidden[:, units:]).astype(BF)
    return jnp.dot(activated, w_out, preferred_element_type=F32).astype(BF)


def tables(meta, slots, before):
    rows = meta.shape[0]
    by_lane = meta[:, :18].astype(F32).T
    target, high, low = by_lane[:6], by_lane[6:12], by_lane[12:18]
    named = (target[None] == slots[:, None, None]).astype(F32)
    member = jnp.sum(named, axis=1)
    weight_high = jnp.sum(named * high[None], axis=1)
    weight_low = jnp.sum(named * low[None], axis=1)
    position = jnp.dot(member.astype(BF), before, preferred_element_type=F32)
    code = jnp.where(member > 0, position, -1.0)
    place = jnp.arange(CAP, dtype=F32)
    hit = code[:, None, :] == place[None, :, None]
    pick = hit.astype(BF).reshape(-1, rows)
    high_mix = jnp.where(hit, weight_high[:, None, :], 0.0).astype(BF).reshape(-1, rows)
    low_mix = jnp.where(hit, weight_low[:, None, :], 0.0).astype(BF).reshape(-1, rows)
    return pick, high_mix, low_mix


def local(stream, gain, routes, route_weights, placement, request_lengths, slot_w_in, slot_w_out):
    row_count, features = stream.shape
    experts = placement.shape[0]
    me = lax.axis_index("req")
    y, z, c = me // (NZ * NC), (me // NC) % NZ, me % NC

    stream_wide = stream.astype(F32)
    inverse = lax.rsqrt(jnp.mean(stream_wide * stream_wide, axis=-1, keepdims=True) + EPS)
    normed = (stream_wide * inverse * gain.astype(F32)).astype(BF)
    total_live = jnp.sum(request_lengths)
    live_rows = jnp.arange(row_count, dtype=jnp.int32) < total_live
    expert_ids = jnp.arange(experts, dtype=jnp.int32)
    target = jnp.sum(jnp.where(routes[:, :, None] == expert_ids, placement, 0), axis=-1)
    target = jnp.where(live_rows[:, None], target, 128).astype(BF)
    high = route_weights.astype(BF)
    low = (route_weights - high.astype(F32)).astype(BF)
    meta = jnp.concatenate(
        [target, high, low, jnp.zeros((row_count, 128 - 18), BF)], axis=1
    )
    block = jnp.concatenate([normed, meta], axis=1)

    dc = jnp.arange(NC)[:, None]
    dy = jnp.arange(NY)[None, :]
    slots = ((((y + dy) % NY) * NZ + z) * NC + (c + dc) % NC).reshape(-1).astype(F32)
    index = jnp.arange(row_count)
    before = (index[:, None] < index[None, :]).astype(BF)

    forward, backward = {0: block}, {0: block}
    for step in range(1, 5):
        forward[step] = _send(forward[step - 1], dz=1)
        if step < 4:
            backward[step] = _send(backward[step - 1], dz=-1)

    chunks = [[forward[0]]] + [[forward[k], backward[k]] for k in (1, 2, 3)] + [[forward[4]]]
    w_in, w_out = slot_w_in[0], slot_w_out[0]
    partials = []
    for blocks in chunks:
        n = len(blocks)
        mixes, picked = [], []
        for held in blocks:
            pick, high_mix, low_mix = tables(held[:, features:], slots, before)
            mixes.append((high_mix, low_mix))
            rows = jnp.dot(pick, held[:, :features], preferred_element_type=F32).astype(BF)
            picked.append(rows.reshape(NC, NY, CAP, features))
        picked = jnp.stack(picked, axis=2)
        other = _send(picked[1], dc=1)
        both = jnp.stack([picked[0], other], axis=1)
        arrived = [both[0]] + [_send(both[d], dy=d) for d in (1, 2, 3)]
        arrived = jnp.stack(arrived, axis=0).reshape(-1, features)
        served = expert_block(arrived, w_in, w_out).reshape(NY, NC, n, CAP, features)
        back = [served[0]] + [_send(served[d], dy=-d) for d in (1, 2, 3)]
        back = jnp.stack(back, axis=0)
        mine = jnp.stack([back[:, 0], _send(back[:, 1], dc=1)], axis=0)
        out = []
        for i in range(n):
            given = mine[:, :, i].reshape(-1, features)
            high_mix, low_mix = mixes[i]
            total = lax.dot_general(high_mix, given, (((0,), (0,)), ((), ())), preferred_element_type=F32)
            total += lax.dot_general(low_mix, given, (((0,), (0,)), ((), ())), preferred_element_type=F32)
            out.append(total)
        partials.append(out)

    ahead = partials[4][0].astype(BF)
    for step in (3, 2, 1):
        ahead = (_send(ahead, dz=-1).astype(F32) + partials[step][0]).astype(BF)
    ahead = _send(ahead, dz=-1)
    behind = partials[3][1].astype(BF)
    for step in (2, 1):
        behind = (_send(behind, dz=1).astype(F32) + partials[step][1]).astype(BF)
    behind = _send(behind, dz=1)
    mixture = partials[0][0] + ahead.astype(F32) + behind.astype(F32)
    return jnp.where(live_rows[:, None], stream_wide + mixture, 0.0).astype(BF)


def solution(mesh):
    in_specs = (
        P(("rep", "req"), None),
        P(),
        P(("rep", "req"), None),
        P(("rep", "req"), None),
        P(),
        P(("rep", "req")),
        P("req", None, None),
        P("req", None, None),
    )
    out_specs = P(("rep", "req"), None)
    return jax.shard_map(local, mesh=mesh, in_specs=in_specs, out_specs=out_specs, check_vma=False)
```

```python
import jax
import jax.numpy as jnp
from jax import lax
from jax.sharding import PartitionSpec as P

EPS = 1e-06
NY, NZ, NC = 4, 8, 2
CAP = 16
BF = jnp.bfloat16
F32 = jnp.float32


def _index(y, z, c):
    return ((y % NY) * NZ + z % NZ) * NC + c % NC


def _shift(dy=0, dz=0, dc=0):
    return [
        (_index(y, z, c), _index(y + dy, z + dz, c + dc))
        for y in range(NY)
        for z in range(NZ)
        for c in range(NC)
    ]


def _send(x, **by):
    return lax.ppermute(x, "req", _shift(**by))


def expert_block(rows, w_in, w_out):
    hidden = jnp.dot(rows, w_in, preferred_element_type=F32)
    units = w_out.shape[0]
    activated = (jax.nn.silu(hidden[:, :units]) * hidden[:, units:]).astype(BF)
    return jnp.dot(activated, w_out, preferred_element_type=F32).astype(BF)


def tables(meta, slots, before):
    rows = meta.shape[0]
    by_lane = meta[:, :18].astype(F32).T
    target, high, low = by_lane[:6], by_lane[6:12], by_lane[12:18]
    named = (target[None] == slots[:, None, None]).astype(F32)
    member = jnp.sum(named, axis=1)
    weight_high = jnp.sum(named * high[None], axis=1)
    weight_low = jnp.sum(named * low[None], axis=1)
    position = jnp.dot(member.astype(BF), before, preferred_element_type=F32)
    code = jnp.where(member > 0, position, -1.0)
    place = jnp.arange(CAP, dtype=F32)
    hit = code[:, None, :] == place[None, :, None]
    pick = hit.astype(BF).reshape(-1, rows)
    high_mix = jnp.where(hit, weight_high[:, None, :], 0.0).astype(BF).reshape(-1, rows)
    low_mix = jnp.where(hit, weight_low[:, None, :], 0.0).astype(BF).reshape(-1, rows)
    return pick, high_mix, low_mix


def local(stream, gain, routes, route_weights, placement, request_lengths, slot_w_in, slot_w_out):
    row_count, features = stream.shape
    experts = placement.shape[0]
    me = lax.axis_index("req")
    y, z, c = me // (NZ * NC), (me // NC) % NZ, me % NC

    stream_wide = stream.astype(F32)
    inverse = lax.rsqrt(jnp.mean(stream_wide * stream_wide, axis=-1, keepdims=True) + EPS)
    normed = (stream_wide * inverse * gain.astype(F32)).astype(BF)
    total_live = jnp.sum(request_lengths)
    live_rows = jnp.arange(row_count, dtype=jnp.int32) < total_live
    expert_ids = jnp.arange(experts, dtype=jnp.int32)
    target = jnp.sum(jnp.where(routes[:, :, None] == expert_ids, placement, 0), axis=-1)
    target = jnp.where(live_rows[:, None], target, 128).astype(BF)
    high = route_weights.astype(BF)
    low = (route_weights - high.astype(F32)).astype(BF)
    meta = jnp.concatenate(
        [target, high, low, jnp.zeros((row_count, 128 - 18), BF)], axis=1
    )
    block = jnp.concatenate([normed, meta], axis=1)

    dy = jnp.arange(NY)[:, None]
    dc = jnp.arange(NC)[None, :]
    slots = ((((y + dy) % NY) * NZ + z) * NC + (c + dc) % NC).reshape(-1).astype(F32)
    index = jnp.arange(row_count)
    before = (index[:, None] < index[None, :]).astype(BF)

    w_in, w_out = slot_w_in[0], slot_w_out[0]
    weights = [(w_in, w_out), (_send(w_in, dc=1), _send(w_out, dc=1))]

    def dispatch(blocks):
        mixes, picked = [], []
        for held in blocks:
            pick, high_mix, low_mix = tables(held[:, features:], slots, before)
            mixes.append((high_mix, low_mix))
            rows = jnp.dot(pick, held[:, :features], preferred_element_type=F32).astype(BF)
            picked.append(rows.reshape(NY, NC, CAP, features))
        ready = [jnp.stack([p[d] for p in picked], axis=1) for d in range(NY)]
        return mixes, ready

    def exchange(ready, sign):
        return [ready[0]] + [_send(ready[d], dy=sign * d) for d in (1, 2, 3)]

    def serve(arrived):
        n = arrived[0].shape[1]
        served = []
        for k in range(NC):
            rows = jnp.concatenate([a[k].reshape(-1, features) for a in arrived], axis=0)
            served.append(expert_block(rows, *weights[k]).reshape(NY, n, CAP, features))
        return [jnp.stack([s[d] for s in served], axis=0) for d in range(NY)]

    def mix(mixes, back):
        out = []
        for i, (high_mix, low_mix) in enumerate(mixes):
            given = jnp.stack([p[:, i] for p in back], axis=0).reshape(-1, features)
            over = (((0,), (0,)), ((), ()))
            total = lax.dot_general(high_mix, given, over, preferred_element_type=F32)
            total += lax.dot_general(low_mix, given, over, preferred_element_type=F32)
            out.append(total)
        return out

    def after(values, *others):
        return lax.optimization_barrier((values, others))[0]

    mixes, served = [], []
    held = [block, block]
    chunk = [block]
    waiting = None
    for step in range(5):
        if step < 3:
            moved = [_send(held[0], dz=1), _send(held[1], dz=-1)]
        elif step == 3:
            moved = [_send(held[0], dz=1)]
        mix_tables, ready = dispatch(chunk)
        mixes.append(mix_tables)
        arrived = exchange(ready, 1)
        if waiting is not None:
            served.append(serve(waiting))
        waiting = arrived
        if step < 4:
            held = after(moved, ready, *served[-1:])
            chunk = held
    served.append(serve(waiting))

    back = exchange(served[4], -1)
    partial = mix(mixes[4], back)
    ahead, behind = partial[0].astype(BF), None
    for step in (3, 2, 1, 0):
        back_sent = exchange(after(served[step], back), -1)
        ahead = _send(ahead, dz=-1)
        if behind is not None:
            behind = _send(behind, dz=1)
        back = back_sent
        partial = mix(mixes[step], back)
        if step == 0:
            mixture = partial[0] + ahead.astype(F32) + behind.astype(F32)
        else:
            ahead = (ahead.astype(F32) + partial[0]).astype(BF)
            behind = partial[1] if behind is None else behind.astype(F32) + partial[1]
            behind = behind.astype(BF)
    return jnp.where(live_rows[:, None], stream_wide + mixture, 0.0).astype(BF)


def solution(mesh):
    in_specs = (
        P(("rep", "req"), None),
        P(),
        P(("rep", "req"), None),
        P(("rep", "req"), None),
        P(),
        P(("rep", "req")),
        P("req", None, None),
        P("req", None, None),
    )
    out_specs = P(("rep", "req"), None)
    return jax.shard_map(local, mesh=mesh, in_specs=in_specs, out_specs=out_specs, check_vma=False)
```

```python
import jax
import jax.numpy as jnp
from jax import lax
from jax.experimental import pallas as pl
from jax.sharding import PartitionSpec as P

EPS = 1e-06
NY, NZ, NC = 4, 8, 2
CAP = 16
BF = jnp.bfloat16
F32 = jnp.float32


def _index(y, z, c):
    return ((y % NY) * NZ + z % NZ) * NC + c % NC


def _shift(dy=0, dz=0, dc=0):
    return [
        (_index(y, z, c), _index(y + dy, z + dz, c + dc))
        for y in range(NY)
        for z in range(NZ)
        for c in range(NC)
    ]


def _send(x, **by):
    return lax.ppermute(x, "req", _shift(**by))


def expert_block(rows, w_in, w_out):
    hidden = jnp.dot(rows, w_in, preferred_element_type=F32)
    units = w_out.shape[0]
    activated = (jax.nn.silu(hidden[:, :units]) * hidden[:, units:]).astype(BF)
    return jnp.dot(activated, w_out, preferred_element_type=F32).astype(BF)


def pick_kernel(slots_ref, *refs):
    n = len(refs) - 4
    blocks, (near_ref, far_ref, high_ref, low_ref) = refs[:n], refs[n:]
    rows = blocks[0].shape[0]
    features = near_ref.shape[-1]
    lane_slot = slots_ref[0:1, :]
    place = (lax.broadcasted_iota(jnp.int32, (1, 128), 1) % CAP).astype(F32)
    earlier = lax.broadcasted_iota(jnp.int32, (rows, rows), 1) < lax.broadcasted_iota(jnp.int32, (rows, rows), 0)
    earlier = earlier.astype(F32).astype(BF)
    for i, block in enumerate(blocks):
        meta = block[:, features:].astype(F32)
        member = jnp.zeros((rows, 128), F32)
        high = jnp.zeros((rows, 128), F32)
        low = jnp.zeros((rows, 128), F32)
        for c in range(6):
            named = meta[:, c : c + 1] == lane_slot
            member = jnp.where(named, 1.0, member)
            high = jnp.where(named, meta[:, 6 + c : 7 + c], high)
            low = jnp.where(named, meta[:, 12 + c : 13 + c], low)
        position = jnp.dot(earlier, member.astype(BF), preferred_element_type=F32)
        hit = jnp.where(position == place, member, 0.0)
        high_ref[i] = (hit * high).astype(BF)
        low_ref[i] = (hit * low).astype(BF)
        picked = jnp.dot(hit.T.astype(BF), block[:, :features], preferred_element_type=F32).astype(BF)
        for d in range(NY):
            near_ref[d, i] = picked[d * CAP : (d + 1) * CAP]
            far_ref[d, i] = picked[(NY + d) * CAP : (NY + d + 1) * CAP]


def pick(slots, blocks, features):
    n = len(blocks)
    rows = blocks[0].shape[0]
    return pl.pallas_call(
        pick_kernel,
        out_shape=[
            jax.ShapeDtypeStruct((NY, n, CAP, features), BF),
            jax.ShapeDtypeStruct((NY, n, CAP, features), BF),
            jax.ShapeDtypeStruct((n, rows, 128), BF),
            jax.ShapeDtypeStruct((n, rows, 128), BF),
        ],
        name="pick",
    )(slots, *blocks)


def local(stream, gain, routes, route_weights, placement, request_lengths, slot_w_in, slot_w_out):
    row_count, features = stream.shape
    experts = placement.shape[0]
    me = lax.axis_index("req")
    y, z, c = me // (NZ * NC), (me // NC) % NZ, me % NC

    stream_wide = stream.astype(F32)
    inverse = lax.rsqrt(jnp.mean(stream_wide * stream_wide, axis=-1, keepdims=True) + EPS)
    normed = (stream_wide * inverse * gain.astype(F32)).astype(BF)
    total_live = jnp.sum(request_lengths)
    live_rows = jnp.arange(row_count, dtype=jnp.int32) < total_live
    expert_ids = jnp.arange(experts, dtype=jnp.int32)
    target = jnp.sum(jnp.where(routes[:, :, None] == expert_ids, placement, 0), axis=-1)
    target = jnp.where(live_rows[:, None], target, 128).astype(BF)
    high = route_weights.astype(BF)
    low = (route_weights - high.astype(F32)).astype(BF)
    meta = jnp.concatenate(
        [target, high, low, jnp.zeros((row_count, 128 - 18), BF)], axis=1
    )
    block = jnp.concatenate([normed, meta], axis=1)

    lane = jnp.arange(128)
    dc, dy = lane // (NY * CAP), (lane // CAP) % NY
    slots = ((((y + dy) % NY) * NZ + z) * NC + (c + dc) % NC).astype(F32)
    slots = jnp.broadcast_to(slots[None], (8, 128))
    w_in, w_out = slot_w_in[0], slot_w_out[0]

    def dispatch(blocks):
        near, far, high_mix, low_mix = pick(slots, blocks, features)
        far = _send(far, dc=1)
        ready = [jnp.stack([near[d], far[d]], axis=0) for d in range(NY)]
        return (high_mix, low_mix), ready

    def exchange(ready, sign):
        return [ready[0]] + [_send(ready[d], dy=sign * d) for d in (1, 2, 3)]

    def serve(arrived):
        rows = jnp.stack(arrived, axis=0)
        served = expert_block(rows.reshape(-1, features), w_in, w_out).reshape(rows.shape)
        return [served[d] for d in range(NY)]

    def mix(mixes, back):
        near = jnp.stack([p[0] for p in back], axis=0)
        far = _send(jnp.stack([p[1] for p in back], axis=0), dc=1)
        out = []
        for i in range(near.shape[1]):
            given = jnp.concatenate([near[:, i], far[:, i]], axis=0).reshape(-1, features)
            total = jnp.dot(mixes[0][i], given, preferred_element_type=F32)
            out.append(total + jnp.dot(mixes[1][i], given, preferred_element_type=F32))
        return out

    def after(values, *others):
        return lax.optimization_barrier((values, others))[0]

    first = [_send(block, dz=1), _send(block, dz=-1)]
    second = [_send(first[0], dz=1), _send(first[1], dz=-1)]
    mixes_a, ready_a = dispatch([block] + first)
    arrived_a = exchange(ready_a, 1)
    second = after(second, ready_a)
    third = [_send(second[0], dz=1), _send(second[1], dz=-1)]
    mixes_b, ready_b = dispatch(second)
    arrived_b = exchange(ready_b, 1)
    third = after(third, ready_b)
    fourth = _send(third[0], dz=1)
    served_a = serve(arrived_a)
    fourth = after(fourth, served_a)
    mixes_c, ready_c = dispatch(third + [fourth])
    arrived_c = exchange(ready_c, 1)
    served_b = serve(arrived_b)
    served_c = serve(after(arrived_c, served_b))

    back_c = exchange(served_c, -1)
    part_c = mix(mixes_c, back_c)
    ahead = _send(part_c[2].astype(BF), dz=-1)
    behind = _send(part_c[1].astype(BF), dz=1)
    back_b = exchange(after(served_b, part_c), -1)
    ahead, behind = after((ahead, behind), back_b)
    part_b = mix(mixes_b, back_b)
    ahead = _send((ahead.astype(F32) + part_c[0]).astype(BF), dz=-1)
    behind = _send((behind.astype(F32) + part_b[1]).astype(BF), dz=1)
    back_a = exchange(after(served_a, part_b), -1)
    ahead = _send((ahead.astype(F32) + part_b[0]).astype(BF), dz=-1)
    part_a = mix(mixes_a, back_a)
    behind = _send((behind.astype(F32) + part_a[2]).astype(BF), dz=1)
    ahead = _send((ahead.astype(F32) + part_a[1]).astype(BF), dz=-1)
    mixture = part_a[0] + ahead.astype(F32) + behind.astype(F32)
    return jnp.where(live_rows[:, None], stream_wide + mixture, 0.0).astype(BF)


def solution(mesh):
    in_specs = (
        P(("rep", "req"), None),
        P(),
        P(("rep", "req"), None),
        P(("rep", "req"), None),
        P(),
        P(("rep", "req")),
        P("req", None, None),
        P("req", None, None),
    )
    out_specs = P(("rep", "req"), None)
    return jax.shard_map(local, mesh=mesh, in_specs=in_specs, out_specs=out_specs, check_vma=False)
```

```python
import jax
import jax.numpy as jnp
from jax import lax
from jax.experimental import pallas as pl
from jax.sharding import PartitionSpec as P

EPS = 1e-06
NY, NZ, NC = 4, 8, 2
CAP = 16
BF = jnp.bfloat16
F32 = jnp.float32


def _index(y, z, c):
    return ((y % NY) * NZ + z % NZ) * NC + c % NC


def _shift(dy=0, dz=0, dc=0):
    return [
        (_index(y, z, c), _index(y + dy, z + dz, c + dc))
        for y in range(NY)
        for z in range(NZ)
        for c in range(NC)
    ]


def _send(x, **by):
    return lax.ppermute(x, "req", _shift(**by))


def expert_block(rows, w_in, w_out):
    hidden = jnp.dot(rows, w_in, preferred_element_type=F32)
    units = w_out.shape[0]
    activated = (jax.nn.silu(hidden[:, :units]) * hidden[:, units:]).astype(BF)
    return jnp.dot(activated, w_out, preferred_element_type=F32).astype(BF)


def pick_kernel(slots_ref, *refs):
    n = len(refs) - 4
    blocks, (near_ref, far_ref, high_ref, low_ref) = refs[:n], refs[n:]
    rows = blocks[0].shape[0]
    features = near_ref.shape[-1]
    lane_slot = slots_ref[0:1, :]
    place = (lax.broadcasted_iota(jnp.int32, (1, 128), 1) % CAP).astype(F32)
    earlier = lax.broadcasted_iota(jnp.int32, (rows, rows), 1) < lax.broadcasted_iota(jnp.int32, (rows, rows), 0)
    earlier = earlier.astype(F32).astype(BF)
    for i, block in enumerate(blocks):
        meta = block[:, features:].astype(F32)
        member = jnp.zeros((rows, 128), F32)
        high = jnp.zeros((rows, 128), F32)
        low = jnp.zeros((rows, 128), F32)
        for c in range(6):
            named = meta[:, c : c + 1] == lane_slot
            member = jnp.where(named, 1.0, member)
            high = jnp.where(named, meta[:, 6 + c : 7 + c], high)
            low = jnp.where(named, meta[:, 12 + c : 13 + c], low)
        position = jnp.dot(earlier, member.astype(BF), preferred_element_type=F32)
        hit = jnp.where(position == place, member, 0.0)
        high_ref[i] = (hit * high).astype(BF)
        low_ref[i] = (hit * low).astype(BF)
        picked = jnp.dot(hit.T.astype(BF), block[:, :features], preferred_element_type=F32).astype(BF)
        for d in range(NY):
            near_ref[d, i] = picked[d * CAP : (d + 1) * CAP]
            far_ref[d, i] = picked[(NY + d) * CAP : (NY + d + 1) * CAP]


def pick(slots, blocks, features):
    n = len(blocks)
    rows = blocks[0].shape[0]
    return pl.pallas_call(
        pick_kernel,
        out_shape=[
            jax.ShapeDtypeStruct((NY, n, CAP, features), BF),
            jax.ShapeDtypeStruct((NY, n, CAP, features), BF),
            jax.ShapeDtypeStruct((n, rows, 128), BF),
            jax.ShapeDtypeStruct((n, rows, 128), BF),
        ],
        name="pick",
    )(slots, *blocks)


def local(stream, gain, routes, route_weights, placement, request_lengths, slot_w_in, slot_w_out):
    row_count, features = stream.shape
    experts = placement.shape[0]
    me = lax.axis_index("req")
    y, z, c = me // (NZ * NC), (me // NC) % NZ, me % NC

    stream_wide = stream.astype(F32)
    inverse = lax.rsqrt(jnp.mean(stream_wide * stream_wide, axis=-1, keepdims=True) + EPS)
    normed = (stream_wide * inverse * gain.astype(F32)).astype(BF)
    total_live = jnp.sum(request_lengths)
    live_rows = jnp.arange(row_count, dtype=jnp.int32) < total_live
    expert_ids = jnp.arange(experts, dtype=jnp.int32)
    target = jnp.sum(jnp.where(routes[:, :, None] == expert_ids, placement, 0), axis=-1)
    target = jnp.where(live_rows[:, None], target, 128).astype(BF)
    high = route_weights.astype(BF)
    low = (route_weights - high.astype(F32)).astype(BF)
    meta = jnp.concatenate(
        [target, high, low, jnp.zeros((row_count, 128 - 18), BF)], axis=1
    )
    block = jnp.concatenate([normed, meta], axis=1)

    lane = jnp.arange(128)
    dc, dy = lane // (NY * CAP), (lane // CAP) % NY
    slots = ((((y + dy) % NY) * NZ + z) * NC + (c + dc) % NC).astype(F32)
    slots = jnp.broadcast_to(slots[None], (8, 128))
    w_in, w_out = slot_w_in[0], slot_w_out[0]

    def dispatch(blocks):
        near, far, high_mix, low_mix = pick(slots, blocks, features)
        far = _send(far, dc=1)
        ready = [jnp.stack([near[d], far[d]], axis=0) for d in range(NY)]
        return (high_mix, low_mix), ready

    def exchange(ready, sign):
        return [ready[0]] + [_send(ready[d], dy=sign * d) for d in (1, 2, 3)]

    def serve(arrived):
        rows = jnp.stack(arrived, axis=0)
        served = expert_block(rows.reshape(-1, features), w_in, w_out).reshape(rows.shape)
        return [served[d] for d in range(NY)]

    def mix(mixes, back):
        near = jnp.stack([p[0] for p in back], axis=0)
        far = _send(jnp.stack([p[1] for p in back], axis=0), dc=1)
        out = []
        for i in range(near.shape[1]):
            given = jnp.concatenate([near[:, i], far[:, i]], axis=0).reshape(-1, features)
            total = jnp.dot(mixes[0][i], given, preferred_element_type=F32)
            out.append(total + jnp.dot(mixes[1][i], given, preferred_element_type=F32))
        return out

    def after(values, *others):
        return lax.optimization_barrier((values, others))[0]

    first = [_send(block, dz=1), _send(block, dz=-1)]
    second = [_send(first[0], dz=1), _send(first[1], dz=-1)]
    mixes_a, ready_a = dispatch([block] + first)
    arrived_a = exchange(ready_a, 1)
    second = after(second, ready_a)
    third = [_send(second[0], dz=1), _send(second[1], dz=-1)]
    mixes_b, ready_b = dispatch(second)
    arrived_b = exchange(ready_b, 1)
    third = after(third, mixes_b, arrived_a)
    fourth = _send(third[0], dz=1)
    fourth = after(fourth, arrived_b)
    mixes_c, ready_c = dispatch(third + [fourth])
    arrived_c = exchange(ready_c, 1)
    served_a = serve(after(arrived_a, ready_c))
    served_b = serve(after(arrived_b, ready_c))
    served_c = serve(after(arrived_c, served_a, served_b))

    back_c = exchange(served_c, -1)
    part_c = mix(mixes_c, back_c)
    ahead = _send(part_c[2].astype(BF), dz=-1)
    behind = _send(part_c[1].astype(BF), dz=1)
    back_b = exchange(after(served_b, part_c), -1)
    ahead, behind = after((ahead, behind), back_b)
    part_b = mix(mixes_b, back_b)
    ahead = (ahead.astype(F32) + part_c[0]).astype(BF)
    behind = (behind.astype(F32) + part_b[1]).astype(BF)
    back_a = after(exchange(after(served_a, back_b), -1), ahead, behind)
    ahead = _send(ahead, dz=-1)
    behind = _send(behind, dz=1)
    ahead = _send((ahead.astype(F32) + part_b[0]).astype(BF), dz=-1)
    part_a = mix(mixes_a, back_a)
    behind = _send((behind.astype(F32) + part_a[2]).astype(BF), dz=1)
    ahead = _send((ahead.astype(F32) + part_a[1]).astype(BF), dz=-1)
    mixture = part_a[0] + ahead.astype(F32) + behind.astype(F32)
    return jnp.where(live_rows[:, None], stream_wide + mixture, 0.0).astype(BF)


def solution(mesh):
    in_specs = (
        P(("rep", "req"), None),
        P(),
        P(("rep", "req"), None),
        P(("rep", "req"), None),
        P(),
        P(("rep", "req")),
        P("req", None, None),
        P("req", None, None),
    )
    out_specs = P(("rep", "req"), None)
    return jax.shard_map(local, mesh=mesh, in_specs=in_specs, out_specs=out_specs, check_vma=False)
```
